32 devices in a mesh: groups: 2 (over y), choice: 16 (over z, x, core).
Axes of the slice: x: 2, y: 2, z: 4, core: 2. Of those that a mesh axis runs over, the one named last changes fastest.
Arguments:
- transitions: bfloat16 [4096, 6, 128, 128], P('choice'), may hold values from -0.21875 to 0.21875
- col_block: int32 [4096, 6], P('choice'), may hold values from 0 to 63
- reward_class: int32 [4, 4096, 128], P(None, 'choice'), may hold values from 0 to 127
- reward_table: bfloat16 [4, 128, 256], P(None, None, 'groups'), parts along dimension 2, may hold values from -6 to 310
- terminal: bfloat16 [8192, 256], P('choice', 'groups'), parts along dimension 1, may hold values from -6 to 6
Outputs:
- values: float32 [8192, 256], P('choice', 'groups'), parts along dimension 1
The draws below stay inside these ranges and needn't reach their ends.
There are 2 independent parts, one for each index of `groups`. The reference program is written for one: setup_inputs(seed, part) draws one part's arguments, and reference() takes and returns one part's arrays. A program takes and returns all parts, laid end to end along the dimension named above; an argument that names none is the same for every part. Nothing has to cross between parts.
All inputs are finite; a program needn't handle non-finite values.
Results may differ from the reference program's by a relative error of at most 0.0013.
Values may be sent and summed in bfloat16 or wider, within the bound.
A program may use at most 256 MiB of HBM per device.

```python
import jax
import jax.numpy as jnp
from jax import lax

NB = 64
BLK = 128
J = 64
K = 6
R = 128
P_SIZE = 128
AGES = 4
STATES = 8192
PAIRS = 4096


def draw_reward_table(key, part):
    base = 1.5 * jax.random.normal(jax.random.fold_in(key, 11), (AGES, R, P_SIZE), jnp.float32)
    base = jnp.clip(base, -6.0, 6.0)
    return base.astype(jnp.bfloat16)


def plant(values, rng, least, high):
    longest = values.shape.index(max(values.shape))
    spots = []
    for shift in (0, 1):
        where = [jax.random.randint(jax.random.fold_in(rng, axis), (), 0, length) for axis, length in enumerate(values.shape)]
        where[longest] = (where[longest] + shift) % values.shape[longest]
        spots.append(tuple(where))
    return values.at[spots[0]].set(least).at[spots[1]].set(high)


def shard_levels(key, extent, shards, low, largest):
    gain = 1.0
    for dim, shards_of in shards:
        draws = jax.random.uniform(jax.random.fold_in(jax.random.fold_in(key, 6), dim), (shards_of,), jnp.float32, low / len(shards), largest / len(shards))
        gain = gain * jnp.repeat(jnp.exp(draws), extent[dim] // shards_of).reshape((-1,) + (1,) * (len(extent) - 1 - dim))
    return gain


def centred(rng, extent, spread, most, pieces=(), kind=jnp.bfloat16):
    result = jax.random.normal(rng, extent, jnp.float32) * spread
    if len(pieces) > 0:
        result = shard_levels(rng, extent, pieces, -0.22, 0.18) * result
    return jnp.clip(result, min=-most, max=most).astype(kind)


def setup_inputs(seed: int = 0, part: int = 0) -> dict:
    keys = jax.random.split(jax.random.key(seed), 6)
    part_splits = jax.random.split(jax.random.fold_in(keys[5], part), 6)
    transitions = centred(keys[0], (PAIRS, K, BLK, BLK), (K * BLK) ** -0.5, 0.21875, ((0, 16),))
    col_block = plant(jax.random.randint(keys[1], (PAIRS, K), 0, NB), jax.random.fold_in(keys[1], 1), 0, NB - 1).astype(jnp.int32)
    reward_class = plant(jax.random.randint(keys[2], (AGES, PAIRS, BLK), 0, R), jax.random.fold_in(keys[2], 1), 0, R - 1).astype(jnp.int32)
    reward_table = draw_reward_table(jax.random.fold_in(jax.random.fold_in(keys[5], part), 71), part)
    terminal = centred(part_splits[4], (STATES, P_SIZE), 1.0, 6.0, ((0, 16),))
    return {"transitions": transitions, "col_block": col_block, "reward_class": reward_class, "reward_table": reward_table, "terminal": terminal}


def reference(transitions, col_block, reward_class, reward_table, terminal):
    next_values = terminal
    current = jnp.zeros((STATES, P_SIZE), jnp.float32)
    for age_index in range(AGES - 1, -1, -1):
        reward_rows = reward_table[age_index].astype(jnp.float32)
        value_blocks = next_values.astype(jnp.float32).reshape(NB, BLK, P_SIZE)
        classes_all = reward_class[age_index]

        def one_row(row_block):
            start = (row_block * J).astype(jnp.int32)
            kernel = lax.dynamic_slice_in_dim(transitions, start, J, 0).astype(jnp.float32)
            column_ids = lax.dynamic_slice_in_dim(col_block, start, J, 0)
            picked = value_blocks[column_ids]
            expected = jnp.einsum("jkab,jkbq->jaq", kernel, picked, precision=lax.Precision.HIGHEST)
            classes = lax.dynamic_slice_in_dim(classes_all, start, J, 0)
            scores = expected + reward_rows[classes]
            highest = jnp.max(scores, axis=0)
            return highest + jnp.log(jnp.sum(jnp.exp(scores - highest[None]), axis=0))

        current = lax.map(one_row, jnp.arange(NB, dtype=jnp.int32)).reshape(STATES, P_SIZE)
        if age_index > 0:
            next_values = current.astype(jnp.bfloat16)
    return current
```

```python
import jax
import jax.numpy as jnp
from jax import lax
from jax.experimental import pallas as pl
from jax.experimental.pallas import tpu as pltpu
from jax.sharding import PartitionSpec as P

J = 64
AGES = 4
STATES = 8192


def partner(array, axis, apart):
    return lax.ppermute(array, axis, [(i, i ^ 1 << apart) for i in range(lax.axis_size(axis))])


def combine(earlier, later):
    highest = jnp.maximum(earlier[0], later[0])
    totals = earlier[1] * jnp.exp(earlier[0] - highest) + later[1] * jnp.exp(later[0] - highest)
    return (highest, totals)


def choice_partials(transitions, col_block, classes, reward_rows, next_values):
    pair_count = transitions.shape[0]
    block_rows = transitions.shape[2]
    columns = next_values.shape[1]
    stacked = next_values.reshape(STATES // block_rows, block_rows, columns)
    picked = jnp.take(stacked, col_block, axis=0)
    expected = jnp.einsum("pkab,pkbq->paq", transitions, picked, preferred_element_type=jnp.float32)
    onehot = (classes[:, :, None] == jnp.arange(reward_rows.shape[0], dtype=jnp.int32)).astype(
        jnp.bfloat16
    )
    reward = jnp.einsum("pbr,rq->pbq", onehot, reward_rows, preferred_element_type=jnp.float32)
    scores = expected + reward
    inner_count = min(J, pair_count)
    grouped = scores.reshape(pair_count // inner_count, inner_count, block_rows, columns)
    highest = jnp.max(grouped, axis=1)
    totals = jnp.sum(jnp.exp(grouped - highest[:, None]), axis=1)
    return (highest.reshape(-1, columns), totals.reshape(-1, columns))


def shards_split(transitions, col_block, reward_class, reward_table, terminal):
    devices = lax.axis_size("choice")
    pair_count = transitions.shape[0]
    inner_count = min(J, pair_count)
    group_size = J // inner_count
    swap_count = group_size.bit_length() - 1
    member_index = lax.axis_index("choice") % group_size
    share_rows = STATES // devices
    next_values = lax.all_gather(terminal, "choice", axis=0, tiled=True)
    result = None
    for age_index in range(AGES - 1, -1, -1):
        highest, totals = choice_partials(
            transitions, col_block, reward_class[age_index], reward_table[age_index], next_values
        )
        for bit_index in range(swap_count):
            incoming = partner((highest, totals), "choice", bit_index)
            highest, totals = combine((highest, totals), incoming)
        block_values = highest + jnp.log(totals)
        if age_index > 0:
            gathered = lax.all_gather(
                block_values.astype(jnp.bfloat16), "choice", axis=0, tiled=True
            )
            spread = gathered.astype(jnp.float32).reshape(
                devices // group_size, group_size, block_values.shape[0], block_values.shape[1]
            )
            next_values = (
                jnp.mean(spread, axis=1).astype(jnp.bfloat16).reshape(STATES, block_values.shape[1])
            )
        else:
            result = lax.dynamic_slice_in_dim(
                block_values, member_index * share_rows, share_rows, 0
            )
    return result


UNROLL = 16
FOLD = 4
LOWEST = -3.0e38
MESH = pl.DeviceIdType.MESH


class Plan:
    def __init__(self, rows):
        self.rows = rows
        self.group = lax.axis_index("groups")
        me = lax.axis_index("choice")
        self.core, self.x, self.z = me % 2, (me // 2) % 2, me // 4
        self.depth = lax.axis_size("choice") // 4
        self.across = self.place(self.z, 1 - self.x, self.core)
        self.beside = self.place(self.z, self.x, 1 - self.core)
        self.mates = [self.place((self.z + d) % self.depth, self.x, self.core) for d in range(1, self.depth)]

    def place(self, z, x, core):
        return z * 4 + x * 2 + core

    def column(self, x, core, b):
        return ((x * 2 + core) * self.rows + b) * self.depth

    def own(self, b):
        return self.column(self.x, self.core, b) + self.z

    def greet(self):
        barrier = pltpu.get_barrier_semaphore()
        near = self.mates + [self.across, self.beside]
        for target in near:
            pl.semaphore_signal(barrier, inc=1, device_id=(self.group, target), device_id_type=MESH)
        pl.semaphore_wait(barrier, len(near))


class Gather:
    def __init__(self, plan, values, side, sems):
        self.plan, self.values, self.side = plan, values, side
        self.send, self.zrecv, self.xrecv, self.brecv = sems

    def copy(self, start, count, recv, target):
        block = self.values.at[pl.ds(start, count)]
        return pltpu.make_async_remote_copy(
            src_ref=block, dst_ref=block, send_sem=self.send.at[self.side], recv_sem=recv,
            device_id=(self.plan.group, target), device_id_type=MESH,
        )

    def take(self, count, sem):
        block = self.values.at[pl.ds(0, count)]
        pltpu.make_async_copy(block, block, sem).wait()

    def spread(self, b):
        p = self.plan
        for target in p.mates:
            self.copy(p.own(b), 1, self.zrecv.at[self.side, b], target).start()

    def along(self, b):
        p = self.plan
        if p.depth > 1:
            self.take(p.depth - 1, self.zrecv.at[self.side, b])
        mine = p.column(p.x, p.core, b)
        self.copy(mine, p.depth, self.xrecv.at[self.side, b], p.across).start()
        self.copy(mine, p.depth, self.brecv.at[self.side], p.beside).start()

    def over(self, b):
        p = self.plan
        self.take(p.depth, self.xrecv.at[self.side, b])
        self.copy(p.column(1 - p.x, p.core, b), p.depth, self.brecv.at[self.side], p.beside).start()

    def finish(self):
        p = self.plan
        self.take(2 * p.rows * p.depth, self.brecv.at[self.side])
        self.take((4 * p.depth - 1) * p.rows, self.send.at[self.side])


def chunk(pair, age, cols_ref, trans, class_ref, table_ref, values, high_ref, total_ref):
    depth, size = trans.shape[1], trans.shape[2]
    types = table_ref.shape[1]
    classes = class_ref[age, pl.ds(pair, UNROLL), :]
    table = table_ref[age]
    kinds = lax.broadcasted_iota(jnp.int32, (types, size), 0)
    for first in range(0, UNROLL, FOLD):
        scores = []
        for i in range(first, first + FOLD):
            left = jnp.concatenate([trans[pair + i, k] for k in range(depth)], axis=1)
            right = jnp.concatenate([values[cols_ref[(pair + i) * depth + k]] for k in range(depth)], axis=0)
            onehot = jnp.where(classes[i : i + 1, :] == kinds, 1.0, 0.0).astype(jnp.bfloat16)
            scores.append(
                jnp.dot(left, right, preferred_element_type=jnp.float32)
                + lax.dot_general(onehot, table, (((0,), (0,)), ((), ())), preferred_element_type=jnp.float32)
            )
        before = high_ref[...]
        high = before
        for s in scores:
            high = jnp.maximum(high, s)
        total = total_ref[...] * jnp.exp(before - high)
        for s in scores:
            total = total + jnp.exp(s - high)
        high_ref[...] = high
        total_ref[...] = total


def whole_kernel(
    cols_ref, trans_ref, class_ref, table_ref, own_ref, out_ref,
    trans, values0, values1, high_ref, total_ref, load, send, zrecv, xrecv, brecv,
):
    rows = own_ref.shape[0]
    steps = J // UNROLL
    plan = Plan(rows)
    values = (values0, values1)
    gathers = [Gather(plan, v, i, (send, zrecv, xrecv, brecv)) for i, v in enumerate(values)]

    def loading(c):
        part = pl.ds(c * UNROLL, UNROLL)
        return pltpu.make_async_copy(trans_ref.at[part], trans.at[part], load.at[c])

    plan.greet()
    first = gathers[0]
    for b in range(rows):
        values0[plan.own(b)] = own_ref[b]
        first.spread(b)

    @pl.loop(0, rows * steps)
    def _(c):
        loading(c).start()

    for b in range(rows):
        first.along(b)
    for b in range(rows):
        first.over(b)
    first.finish()

    for turn in range(AGES):
        age = AGES - 1 - turn
        held = values[turn % 2]
        ahead = gathers[(turn + 1) % 2]
        last = turn == AGES - 1

        @pl.loop(0, rows)
        def _(r):
            high_ref[...] = jnp.full_like(high_ref, LOWEST)
            total_ref[...] = jnp.zeros_like(total_ref)

            @pl.loop(0, steps)
            def _(q):
                if turn == 0:
                    loading(r * steps + q).wait()
                chunk((r * steps + q) * UNROLL, age, cols_ref, trans, class_ref, table_ref, held, high_ref, total_ref)
                if not last:

                    @pl.when((r > 0) & (q == 0))
                    def _():
                        ahead.along(r - 1)

                    @pl.when((r > 0) & (q == steps // 2))
                    def _():
                        ahead.over(r - 1)

            done = high_ref[...] + jnp.log(total_ref[...])
            if last:
                out_ref[r] = done
            else:
                ahead.values[plan.own(r)] = done.astype(jnp.bfloat16)
                ahead.spread(r)

        if not last:
            ahead.along(rows - 1)
            ahead.over(rows - 1)
            ahead.finish()


def shards_whole(transitions, col_block, reward_class, reward_table, terminal):
    pairs, depth, size, _ = transitions.shape
    columns = terminal.shape[1]
    devices = lax.axis_size("choice")
    blocks = devices * (terminal.shape[0] // size)
    rows = pairs // J
    ranks = devices // 4
    owner, b = col_block // rows, col_block % rows
    cols = ((owner % 4) * rows + b) * ranks + owner // 4
    vmem = pl.BlockSpec(memory_space=pltpu.VMEM)
    out = pl.pallas_call(
        whole_kernel,
        out_shape=jax.ShapeDtypeStruct((rows, size, columns), jnp.float32),
        in_specs=[
            pl.BlockSpec(memory_space=pltpu.SMEM), pl.BlockSpec(memory_space=pl.ANY), vmem, vmem, vmem,
        ],
        out_specs=vmem,
        scratch_shapes=[
            pltpu.VMEM(transitions.shape, jnp.bfloat16),
            pltpu.VMEM((blocks, size, columns), jnp.bfloat16),
            pltpu.VMEM((blocks, size, columns), jnp.bfloat16),
            pltpu.VMEM((size, columns), jnp.float32),
            pltpu.VMEM((size, columns), jnp.float32),
            pltpu.SemaphoreType.DMA((pairs // UNROLL,)),
            pltpu.SemaphoreType.DMA((2,)),
            pltpu.SemaphoreType.DMA((2, rows)),
            pltpu.SemaphoreType.DMA((2, rows)),
            pltpu.SemaphoreType.DMA((2,)),
        ],
        compiler_params=pltpu.CompilerParams(
            collective_id=0, has_side_effects=True, vmem_limit_bytes=58 << 20
        ),
        cost_estimate=pl.CostEstimate(
            flops=2 * AGES * pairs * (depth * size + reward_table.shape[1]) * size * columns,
            bytes_accessed=transitions.size * 2,
            transcendentals=AGES * pairs * size * columns,
        ),
    )(cols.reshape(-1), transitions, reward_class, reward_table, terminal.reshape(rows, size, columns))
    return out.reshape(terminal.shape)


def shards(transitions, col_block, reward_class, reward_table, terminal):
    whole = transitions.shape[0] % J == 0 and lax.axis_size("choice") % 4 == 0
    body = shards_whole if whole else shards_split
    return body(transitions, col_block, reward_class, reward_table, terminal)


def solution(mesh):
    return jax.shard_map(
        shards,
        mesh=mesh,
        in_specs=(
            P("choice", None, None, None),
            P("choice", None),
            P(None, "choice", None),
            P(None, None, "groups"),
            P("choice", "groups"),
        ),
        out_specs=P("choice", "groups"),
        check_vma=False,
    )
```

```python
import jax
import jax.numpy as jnp
from jax import lax
from jax.experimental import pallas as pl
from jax.experimental.pallas import tpu as pltpu
from jax.sharding import PartitionSpec as P

J = 64
AGES = 4
STATES = 8192


def partner(array, axis, apart):
    return lax.ppermute(array, axis, [(i, i ^ 1 << apart) for i in range(lax.axis_size(axis))])


def combine(earlier, later):
    highest = jnp.maximum(earlier[0], later[0])
    totals = earlier[1] * jnp.exp(earlier[0] - highest) + later[1] * jnp.exp(later[0] - highest)
    return (highest, totals)


def choice_partials(transitions, col_block, classes, reward_rows, next_values):
    pair_count = transitions.shape[0]
    block_rows = transitions.shape[2]
    columns = next_values.shape[1]
    stacked = next_values.reshape(STATES // block_rows, block_rows, columns)
    picked = jnp.take(stacked, col_block, axis=0)
    expected = jnp.einsum("pkab,pkbq->paq", transitions, picked, preferred_element_type=jnp.float32)
    onehot = (classes[:, :, None] == jnp.arange(reward_rows.shape[0], dtype=jnp.int32)).astype(
        jnp.bfloat16
    )
    reward = jnp.einsum("pbr,rq->pbq", onehot, reward_rows, preferred_element_type=jnp.float32)
    scores = expected + reward
    inner_count = min(J, pair_count)
    grouped = scores.reshape(pair_count // inner_count, inner_count, block_rows, columns)
    highest = jnp.max(grouped, axis=1)
    totals = jnp.sum(jnp.exp(grouped - highest[:, None]), axis=1)
    return (highest.reshape(-1, columns), totals.reshape(-1, columns))


def shards_split(transitions, col_block, reward_class, reward_table, terminal):
    devices = lax.axis_size("choice")
    pair_count = transitions.shape[0]
    inner_count = min(J, pair_count)
    group_size = J // inner_count
    swap_count = group_size.bit_length() - 1
    member_index = lax.axis_index("choice") % group_size
    share_rows = STATES // devices
    next_values = lax.all_gather(terminal, "choice", axis=0, tiled=True)
    result = None
    for age_index in range(AGES - 1, -1, -1):
        highest, totals = choice_partials(
            transitions, col_block, reward_class[age_index], reward_table[age_index], next_values
        )
        for bit_index in range(swap_count):
            incoming = partner((highest, totals), "choice", bit_index)
            highest, totals = combine((highest, totals), incoming)
        block_values = highest + jnp.log(totals)
        if age_index > 0:
            gathered = lax.all_gather(
                block_values.astype(jnp.bfloat16), "choice", axis=0, tiled=True
            )
            spread = gathered.astype(jnp.float32).reshape(
                devices // group_size, group_size, block_values.shape[0], block_values.shape[1]
            )
            next_values = (
                jnp.mean(spread, axis=1).astype(jnp.bfloat16).reshape(STATES, block_values.shape[1])
            )
        else:
            result = lax.dynamic_slice_in_dim(
                block_values, member_index * share_rows, share_rows, 0
            )
    return result


UNROLL = 32
FOLD = 2
ZLAG = 3
XLAG = 5
LOWEST = -3.0e38
MESH = pl.DeviceIdType.MESH


class Plan:
    def __init__(self, rows):
        self.rows = rows
        self.group = lax.axis_index("groups")
        me = lax.axis_index("choice")
        self.core, self.x, self.z = me % 2, (me // 2) % 2, me // 4
        self.depth = lax.axis_size("choice") // 4
        self.across = self.place(self.z, 1 - self.x, self.core)
        self.beside = self.place(self.z, self.x, 1 - self.core)
        self.mates = [self.place((self.z + d) % self.depth, self.x, self.core) for d in range(1, self.depth)]

    def place(self, z, x, core):
        return z * 4 + x * 2 + core

    def column(self, x, core, b):
        return ((x * 2 + core) * self.rows + b) * self.depth

    def own(self, b):
        return self.column(self.x, self.core, b) + self.z

    def greet(self):
        barrier = pltpu.get_barrier_semaphore()
        near = self.mates + [self.across, self.beside]
        for target in near:
            pl.semaphore_signal(barrier, inc=1, device_id=(self.group, target), device_id_type=MESH)
        pl.semaphore_wait(barrier, len(near))


class Gather:
    def __init__(self, plan, values, side, sems):
        self.plan, self.values, self.side = plan, values, side
        self.send, self.zrecv, self.xrecv, self.zlast, self.xlast, self.brecv = sems

    def copy(self, start, count, recv, target):
        block = self.values.at[pl.ds(start, count)]
        return pltpu.make_async_remote_copy(
            src_ref=block, dst_ref=block, send_sem=self.send.at[self.side], recv_sem=recv,
            device_id=(self.plan.group, target), device_id_type=MESH,
        )

    def take(self, count, sem):
        block = self.values.at[pl.ds(0, count)]
        pltpu.make_async_copy(block, block, sem).wait()

    def aside(self, start, count):
        self.copy(start, count, self.brecv.at[self.side], self.plan.beside).start()

    def spread(self, b):
        p = self.plan
        for target in p.mates:
            self.copy(p.own(b), 1, self.zrecv.at[self.side, b], target).start()

    def along(self, b):
        p = self.plan
        if p.depth > 1:
            self.take(p.depth - 1, self.zrecv.at[self.side, b])
        mine = p.column(p.x, p.core, b)
        self.copy(mine, p.depth, self.xrecv.at[self.side, b], p.across).start()
        self.aside(mine, p.depth)

    def over(self, b):
        p = self.plan
        self.take(p.depth, self.xrecv.at[self.side, b])
        self.aside(p.column(1 - p.x, p.core, b), p.depth)

    def last_spread(self):
        p = self.plan
        own = p.own(p.rows - 1)
        self.copy(own, 1, self.xlast.at[self.side, 0], p.across).start()
        for i, target in enumerate(p.mates):
            self.copy(own, 1, self.zlast.at[self.side, i], target).start()
        self.aside(own, 1)

    def last_along(self, i):
        p = self.plan
        self.take(1, self.zlast.at[self.side, i])
        block = p.column(p.x, p.core, p.rows - 1) + (p.z + p.depth - 1 - i) % p.depth
        self.copy(block, 1, self.xlast.at[self.side, i + 1], p.across).start()
        self.aside(block, 1)

    def last_over(self, i):
        p = self.plan
        self.take(1, self.xlast.at[self.side, i])
        block = p.column(1 - p.x, p.core, p.rows - 1) + (p.z + p.depth - i) % p.depth
        self.aside(block, 1)

    def last_all(self):
        p = self.plan
        for i in range(p.depth - 1):
            self.last_along(i)
        for i in range(p.depth):
            self.last_over(i)

    def finish(self):
        p = self.plan
        self.take(2 * p.rows * p.depth, self.brecv.at[self.side])
        self.take((4 * p.depth - 1) * p.rows, self.send.at[self.side])


def chunk(pair, age, cols_ref, trans, class_ref, table_ref, values, high_ref, total_ref):
    depth, size = trans.shape[1], trans.shape[2]
    types = table_ref.shape[1]
    classes = class_ref[age, pl.ds(pair, UNROLL), :]
    table = table_ref[age]
    kinds = lax.broadcasted_iota(jnp.int32, (types, size), 0)
    for first in range(0, UNROLL, FOLD):
        scores = []
        for i in range(first, first + FOLD):
            left = jnp.concatenate([trans[pair + i, k] for k in range(depth)], axis=1)
            right = jnp.concatenate([values[cols_ref[(pair + i) * depth + k]] for k in range(depth)], axis=0)
            onehot = jnp.where(classes[i : i + 1, :] == kinds, 1.0, 0.0).astype(jnp.bfloat16)
            scores.append(
                jnp.dot(left, right, preferred_element_type=jnp.float32)
                + lax.dot_general(onehot, table, (((0,), (0,)), ((), ())), preferred_element_type=jnp.float32)
            )
        before = high_ref[...]
        high = before
        for s in scores:
            high = jnp.maximum(high, s)
        total = total_ref[...] * jnp.exp(before - high)
        for s in scores:
            total = total + jnp.exp(s - high)
        high_ref[...] = high
        total_ref[...] = total


def whole_kernel(
    cols_ref, trans_ref, class_ref, table_ref, own_ref, out_ref,
    trans, values0, values1, high_ref, total_ref, load, send, zrecv, xrecv, zlast, xlast, brecv,
):
    rows = own_ref.shape[0]
    steps = J // UNROLL
    plan = Plan(rows)
    values = (values0, values1)
    gathers = [Gather(plan, v, i, (send, zrecv, xrecv, zlast, xlast, brecv)) for i, v in enumerate(values)]

    def loading(c):
        part = pl.ds(c * UNROLL, UNROLL)
        return pltpu.make_async_copy(trans_ref.at[part], trans.at[part], load.at[c])

    plan.greet()
    first = gathers[0]

    def begin(b):
        values0[plan.own(b)] = own_ref[b]
        if b == rows - 1:
            first.last_spread()
        else:
            first.spread(b)

    for b in range(min(2, rows)):
        begin(b)

    @pl.loop(0, rows * steps)
    def _(c):
        loading(c).start()

    for b in range(rows - 1):
        first.along(b)
        if b + 2 < rows:
            begin(b + 2)
        if b > 0:
            first.over(b - 1)
    if rows > 1:
        first.over(rows - 2)
    first.last_all()
    first.finish()

    for turn in range(AGES):
        age = AGES - 1 - turn
        held = values[turn % 2]
        ahead = gathers[(turn + 1) % 2]
        last = turn == AGES - 1

        @pl.loop(0, rows)
        def _(r):
            high_ref[...] = jnp.full_like(high_ref, LOWEST)
            total_ref[...] = jnp.zeros_like(total_ref)

            @pl.loop(0, steps)
            def _(q):
                if turn == 0:
                    loading(r * steps + q).wait()
                chunk((r * steps + q) * UNROLL, age, cols_ref, trans, class_ref, table_ref, held, high_ref, total_ref)
                if not last:
                    at = r * steps + q

                    @pl.when((at % steps == (steps - 1 + ZLAG) % steps) & (at >= steps - 1 + ZLAG))
                    def _():
                        ahead.along((at - ZLAG) // steps)

                    @pl.when((at % steps == (steps - 1 + XLAG) % steps) & (at >= steps - 1 + XLAG))
                    def _():
                        ahead.over((at - XLAG) // steps)

            done = high_ref[...] + jnp.log(total_ref[...])
            if last:
                out_ref[r] = done
            else:
                ahead.values[plan.own(r)] = done.astype(jnp.bfloat16)

                @pl.when(r < rows - 1)
                def _():
                    ahead.spread(r)

                @pl.when(r == rows - 1)
                def _():
                    ahead.last_spread()

        if not last:
            ends = [steps * (b + 1) - 1 for b in range(rows - 1)]
            final = rows * steps - 1
            for b, end in enumerate(ends):
                if end + ZLAG > final:
                    ahead.along(b)
            for b, end in enumerate(ends):
                if end + XLAG > final:
                    ahead.over(b)
            ahead.last_all()
            ahead.finish()


def shards_whole(transitions, col_block, reward_class, reward_table, terminal):
    pairs, depth, size, _ = transitions.shape
    columns = terminal.shape[1]
    devices = lax.axis_size("choice")
    blocks = devices * (terminal.shape[0] // size)
    rows = pairs // J
    ranks = devices // 4
    owner, b = col_block // rows, col_block % rows
    cols = ((owner % 4) * rows + b) * ranks + owner // 4
    vmem = pl.BlockSpec(memory_space=pltpu.VMEM)
    out = pl.pallas_call(
        whole_kernel,
        out_shape=jax.ShapeDtypeStruct((rows, size, columns), jnp.float32),
        in_specs=[
            pl.BlockSpec(memory_space=pltpu.SMEM), pl.BlockSpec(memory_space=pl.ANY), vmem, vmem, vmem,
        ],
        out_specs=vmem,
        scratch_shapes=[
            pltpu.VMEM(transitions.shape, jnp.bfloat16),
            pltpu.VMEM((blocks, size, columns), jnp.bfloat16),
            pltpu.VMEM((blocks, size, columns), jnp.bfloat16),
            pltpu.VMEM((size, columns), jnp.float32),
            pltpu.VMEM((size, columns), jnp.float32),
            pltpu.SemaphoreType.DMA((pairs // UNROLL,)),
            pltpu.SemaphoreType.DMA((2,)),
            pltpu.SemaphoreType.DMA((2, rows)),
            pltpu.SemaphoreType.DMA((2, rows)),
            pltpu.SemaphoreType.DMA((2, ranks)),
            pltpu.SemaphoreType.DMA((2, ranks)),
            pltpu.SemaphoreType.DMA((2,)),
        ],
        compiler_params=pltpu.CompilerParams(
            collective_id=0, has_side_effects=True, vmem_limit_bytes=58 << 20
        ),
        cost_estimate=pl.CostEstimate(
            flops=2 * AGES * pairs * (depth * size + reward_table.shape[1]) * size * columns,
            bytes_accessed=transitions.size * 2,
            transcendentals=AGES * pairs * size * columns,
        ),
    )(cols.reshape(-1), transitions, reward_class, reward_table, terminal.reshape(rows, size, columns))
    return out.reshape(terminal.shape)


def shards(transitions, col_block, reward_class, reward_table, terminal):
    whole = transitions.shape[0] % J == 0 and lax.axis_size("choice") % 4 == 0
    body = shards_whole if whole else shards_split
    return body(transitions, col_block, reward_class, reward_table, terminal)


def solution(mesh):
    return jax.shard_map(
        shards,
        mesh=mesh,
        in_specs=(
            P("choice", None, None, None),
            P("choice", None),
            P(None, "choice", None),
            P(None, None, "groups"),
            P("choice", "groups"),
        ),
        out_specs=P("choice", "groups"),
        check_vma=False,
    )
```

```python
import jax
import jax.numpy as jnp
from jax import lax
from jax.experimental import pallas as pl
from jax.experimental.pallas import tpu as pltpu
from jax.sharding import PartitionSpec as P

J = 64
AGES = 4
STATES = 8192


def partner(array, axis, apart):
    return lax.ppermute(array, axis, [(i, i ^ 1 << apart) for i in range(lax.axis_size(axis))])


def combine(earlier, later):
    highest = jnp.maximum(earlier[0], later[0])
    totals = earlier[1] * jnp.exp(earlier[0] - highest) + later[1] * jnp.exp(later[0] - highest)
    return (highest, totals)


def choice_partials(transitions, col_block, classes, reward_rows, next_values):
    pair_count = transitions.shape[0]
    block_rows = transitions.shape[2]
    columns = next_values.shape[1]
    stacked = next_values.reshape(STATES // block_rows, block_rows, columns)
    picked = jnp.take(stacked, col_block, axis=0)
    expected = jnp.einsum("pkab,pkbq->paq", transitions, picked, preferred_element_type=jnp.float32)
    onehot = (classes[:, :, None] == jnp.arange(reward_rows.shape[0], dtype=jnp.int32)).astype(
        jnp.bfloat16
    )
    reward = jnp.einsum("pbr,rq->pbq", onehot, reward_rows, preferred_element_type=jnp.float32)
    scores = expected + reward
    inner_count = min(J, pair_count)
    grouped = scores.reshape(pair_count // inner_count, inner_count, block_rows, columns)
    highest = jnp.max(grouped, axis=1)
    totals = jnp.sum(jnp.exp(grouped - highest[:, None]), axis=1)
    return (highest.reshape(-1, columns), totals.reshape(-1, columns))


def shards_split(transitions, col_block, reward_class, reward_table, terminal):
    devices = lax.axis_size("choice")
    pair_count = transitions.shape[0]
    inner_count = min(J, pair_count)
    group_size = J // inner_count
    swap_count = group_size.bit_length() - 1
    member_index = lax.axis_index("choice") % group_size
    share_rows = STATES // devices
    next_values = lax.all_gather(terminal, "choice", axis=0, tiled=True)
    result = None
    for age_index in range(AGES - 1, -1, -1):
        highest, totals = choice_partials(
            transitions, col_block, reward_class[age_index], reward_table[age_index], next_values
        )
        for bit_index in range(swap_count):
            incoming = partner((highest, totals), "choice", bit_index)
            highest, totals = combine((highest, totals), incoming)
        block_values = highest + jnp.log(totals)
        if age_index > 0:
            gathered = lax.all_gather(
                block_values.astype(jnp.bfloat16), "choice", axis=0, tiled=True
            )
            spread = gathered.astype(jnp.float32).reshape(
                devices // group_size, group_size, block_values.shape[0], block_values.shape[1]
            )
            next_values = (
                jnp.mean(spread, axis=1).astype(jnp.bfloat16).reshape(STATES, block_values.shape[1])
            )
        else:
            result = lax.dynamic_slice_in_dim(
                block_values, member_index * share_rows, share_rows, 0
            )
    return result


UNROLL = 32
FOLD = 2
ZLAG = 3
XLAG = 5
LOWEST = -3.0e38
MESH = pl.DeviceIdType.MESH


class Plan:
    def __init__(self, rows):
        self.rows = rows
        self.group = lax.axis_index("groups")
        me = lax.axis_index("choice")
        self.core, self.x, self.z = me % 2, (me // 2) % 2, me // 4
        self.depth = lax.axis_size("choice") // 4
        self.across = self.place(self.z, 1 - self.x, self.core)
        self.beside = self.place(self.z, self.x, 1 - self.core)
        self.mates = [self.place((self.z + d) % self.depth, self.x, self.core) for d in range(1, self.depth)]

    def place(self, z, x, core):
        return z * 4 + x * 2 + core

    def column(self, x, core, b):
        return ((x * 2 + core) * self.rows + b) * self.depth

    def own(self, b):
        return self.column(self.x, self.core, b) + self.z

    def greet(self):
        barrier = pltpu.get_barrier_semaphore()
        near = self.mates + [self.across, self.beside]
        for target in near:
            pl.semaphore_signal(barrier, inc=1, device_id=(self.group, target), device_id_type=MESH)
        pl.semaphore_wait(barrier, len(near))


class Gather:
    def __init__(self, plan, values, side, sems):
        self.plan, self.values, self.side = plan, values, side
        self.send, self.zrecv, self.xrecv, self.zlast, self.xlast, self.brecv = sems

    def copy(self, start, count, recv, target):
        block = self.values.at[pl.ds(start, count)]
        return pltpu.make_async_remote_copy(
            src_ref=block, dst_ref=block, send_sem=self.send.at[self.side], recv_sem=recv,
            device_id=(self.plan.group, target), device_id_type=MESH,
        )

    def take(self, count, sem):
        block = self.values.at[pl.ds(0, count)]
        pltpu.make_async_copy(block, block, sem).wait()

    def aside(self, start, count):
        self.copy(start, count, self.brecv.at[self.side], self.plan.beside).start()

    def spread(self, b):
        p = self.plan
        for target in p.mates:
            self.copy(p.own(b), 1, self.zrecv.at[self.side, b], target).start()

    def along(self, b):
        p = self.plan
        if p.depth > 1:
            self.take(p.depth - 1, self.zrecv.at[self.side, b])
        mine = p.column(p.x, p.core, b)
        self.copy(mine, p.depth, self.xrecv.at[self.side, b], p.across).start()
        self.aside(mine, p.depth)

    def over(self, b):
        p = self.plan
        self.take(p.depth, self.xrecv.at[self.side, b])
        self.aside(p.column(1 - p.x, p.core, b), p.depth)

    def last_spread(self):
        p = self.plan
        own = p.own(p.rows - 1)
        self.copy(own, 1, self.xlast.at[self.side, 0], p.across).start()
        for i, target in enumerate(p.mates):
            self.copy(own, 1, self.zlast.at[self.side, i], target).start()
        self.aside(own, 1)

    def last_along(self, i):
        p = self.plan
        self.take(1, self.zlast.at[self.side, i])
        block = p.column(p.x, p.core, p.rows - 1) + (p.z + p.depth - 1 - i) % p.depth
        self.copy(block, 1, self.xlast.at[self.side, i + 1], p.across).start()
        self.aside(block, 1)

    def last_over(self, i):
        p = self.plan
        self.take(1, self.xlast.at[self.side, i])
        block = p.column(1 - p.x, p.core, p.rows - 1) + (p.z + p.depth - i) % p.depth
        self.aside(block, 1)

    def finish(self):
        p = self.plan
        self.take(2 * p.rows * p.depth, self.brecv.at[self.side])
        self.take((4 * p.depth - 1) * p.rows, self.send.at[self.side])


def chunk(pair, age, cols_ref, trans, class_ref, table_ref, values, high_ref, total_ref):
    depth, size = trans.shape[1], trans.shape[2]
    types = table_ref.shape[1]
    classes = class_ref[age, pl.ds(pair, UNROLL), :]
    table = table_ref[age]
    kinds = lax.broadcasted_iota(jnp.int32, (types, size), 0)
    for first in range(0, UNROLL, FOLD):
        scores = []
        for i in range(first, first + FOLD):
            left = jnp.concatenate([trans[pair + i, k] for k in range(depth)], axis=1)
            right = jnp.concatenate([values[cols_ref[(pair + i) * depth + k]] for k in range(depth)], axis=0)
            onehot = jnp.where(classes[i : i + 1, :] == kinds, 1.0, 0.0).astype(jnp.bfloat16)
            scores.append(
                jnp.dot(left, right, preferred_element_type=jnp.float32)
                + lax.dot_general(onehot, table, (((0,), (0,)), ((), ())), preferred_element_type=jnp.float32)
            )
        before = high_ref[...]
        high = before
        for s in scores:
            high = jnp.maximum(high, s)
        total = total_ref[...] * jnp.exp(before - high)
        for s in scores:
            total = total + jnp.exp(s - high)
        high_ref[...] = high
        total_ref[...] = total


def whole_kernel(
    cols_ref, trans_ref, class_ref, table_ref, own_ref, out_ref,
    trans, values0, values1, high_ref, total_ref, load, send, zrecv, xrecv, zlast, xlast, brecv,
):
    rows = own_ref.shape[0]
    steps = J // UNROLL
    plan = Plan(rows)
    values = (values0, values1)
    gathers = [Gather(plan, v, i, (send, zrecv, xrecv, zlast, xlast, brecv)) for i, v in enumerate(values)]

    def loading(c):
        part = pl.ds(c * UNROLL, UNROLL)
        return pltpu.make_async_copy(trans_ref.at[part], trans.at[part], load.at[c])

    plan.greet()
    first = gathers[0]

    def begin(b):
        values0[plan.own(b)] = own_ref[b]
        if b == rows - 1:
            first.last_spread()
        else:
            first.spread(b)

    for b in range(min(2, rows)):
        begin(b)

    @pl.loop(0, rows * steps)
    def _(c):
        loading(c).start()

    for b in range(rows - 1):
        first.along(b)
        if b + 2 < rows:
            begin(b + 2)
        if b > 0:
            first.over(b - 1)
    for i in range(plan.depth - 1):
        first.last_along(i)
    if rows > 1:
        first.over(rows - 2)
    for i in range(plan.depth):
        first.last_over(i)
    first.finish()

    for turn in range(AGES):
        age = AGES - 1 - turn
        held = values[turn % 2]
        ahead = gathers[(turn + 1) % 2]
        last = turn == AGES - 1

        @pl.loop(0, rows)
        def _(r):
            high_ref[...] = jnp.full_like(high_ref, LOWEST)
            total_ref[...] = jnp.zeros_like(total_ref)

            @pl.loop(0, steps)
            def _(q):
                if turn == 0:
                    loading(r * steps + q).wait()
                chunk((r * steps + q) * UNROLL, age, cols_ref, trans, class_ref, table_ref, held, high_ref, total_ref)
                if not last:
                    at = r * steps + q

                    @pl.when((at % steps == (steps - 1 + ZLAG) % steps) & (at >= steps - 1 + ZLAG))
                    def _():
                        ahead.along((at - ZLAG) // steps)

                    @pl.when((at % steps == (steps - 1 + XLAG) % steps) & (at >= steps - 1 + XLAG))
                    def _():
                        ahead.over((at - XLAG) // steps)

            done = high_ref[...] + jnp.log(total_ref[...])
            if last:
                out_ref[r] = done
            else:
                ahead.values[plan.own(r)] = done.astype(jnp.bfloat16)

                @pl.when(r < rows - 1)
                def _():
                    ahead.spread(r)

                @pl.when(r == rows - 1)
                def _():
                    ahead.last_spread()

        if not last:
            ends = [steps * (b + 1) - 1 for b in range(rows - 1)]
            final = rows * steps - 1
            for b, end in enumerate(ends):
                if end + ZLAG > final:
                    ahead.along(b)
            for i in range(plan.depth - 1):
                ahead.last_along(i)
            for b, end in enumerate(ends):
                if end + XLAG > final:
                    ahead.over(b)
            for i in range(plan.depth):
                ahead.last_over(i)
            ahead.finish()


def shards_whole(transitions, col_block, reward_class, reward_table, terminal):
    pairs, depth, size, _ = transitions.shape
    columns = terminal.shape[1]
    devices = lax.axis_size("choice")
    blocks = devices * (terminal.shape[0] // size)
    rows = pairs // J
    ranks = devices // 4
    owner, b = col_block // rows, col_block % rows
    cols = ((owner % 4) * rows + b) * ranks + owner // 4
    vmem = pl.BlockSpec(memory_space=pltpu.VMEM)
    out = pl.pallas_call(
        whole_kernel,
        out_shape=jax.ShapeDtypeStruct((rows, size, columns), jnp.float32),
        in_specs=[
            pl.BlockSpec(memory_space=pltpu.SMEM), pl.BlockSpec(memory_space=pl.ANY), vmem, vmem, vmem,
        ],
        out_specs=vmem,
        scratch_shapes=[
            pltpu.VMEM(transitions.shape, jnp.bfloat16),
            pltpu.VMEM((blocks, size, columns), jnp.bfloat16),
            pltpu.VMEM((blocks, size, columns), jnp.bfloat16),
            pltpu.VMEM((size, columns), jnp.float32),
            pltpu.VMEM((size, columns), jnp.float32),
            pltpu.SemaphoreType.DMA((pairs // UNROLL,)),
            pltpu.SemaphoreType.DMA((2,)),
            pltpu.SemaphoreType.DMA((2, rows)),
            pltpu.SemaphoreType.DMA((2, rows)),
            pltpu.SemaphoreType.DMA((2, ranks)),
            pltpu.SemaphoreType.DMA((2, ranks)),
            pltpu.SemaphoreType.DMA((2,)),
        ],
        compiler_params=pltpu.CompilerParams(
            collective_id=0, has_side_effects=True, vmem_limit_bytes=58 << 20
        ),
        cost_estimate=pl.CostEstimate(
            flops=2 * AGES * pairs * (depth * size + reward_table.shape[1]) * size * columns,
            bytes_accessed=transitions.size * 2,
            transcendentals=AGES * pairs * size * columns,
        ),
    )(cols.reshape(-1), transitions, reward_class, reward_table, terminal.reshape(rows, size, columns))
    return out.reshape(terminal.shape)


def shards(transitions, col_block, reward_class, reward_table, terminal):
    whole = transitions.shape[0] % J == 0 and lax.axis_size("choice") % 4 == 0
    body = shards_whole if whole else shards_split
    return body(transitions, col_block, reward_class, reward_table, terminal)


def solution(mesh):
    return jax.shard_map(
        shards,
        mesh=mesh,
        in_specs=(
            P("choice", None, None, None),
            P("choice", None),
            P(None, "choice", None),
            P(None, None, "groups"),
            P("choice", "groups"),
        ),
        out_specs=P("choice", "groups"),
        check_vma=False,
    )
```

```python
import jax
import jax.numpy as jnp
from jax import lax
from jax.experimental import pallas as pl
from jax.experimental.pallas import tpu as pltpu
from jax.sharding import PartitionSpec as P

J = 64
AGES = 4
STATES = 8192


def partner(array, axis, apart):
    return lax.ppermute(array, axis, [(i, i ^ 1 << apart) for i in range(lax.axis_size(axis))])


def combine(earlier, later):
    highest = jnp.maximum(earlier[0], later[0])
    totals = earlier[1] * jnp.exp(earlier[0] - highest) + later[1] * jnp.exp(later[0] - highest)
    return (highest, totals)


def choice_partials(transitions, col_block, classes, reward_rows, next_values):
    pair_count = transitions.shape[0]
    block_rows = transitions.shape[2]
    columns = next_values.shape[1]
    stacked = next_values.reshape(STATES // block_rows, block_rows, columns)
    picked = jnp.take(stacked, col_block, axis=0)
    expected = jnp.einsum("pkab,pkbq->paq", transitions, picked, preferred_element_type=jnp.float32)
    onehot = (classes[:, :, None] == jnp.arange(reward_rows.shape[0], dtype=jnp.int32)).astype(
        jnp.bfloat16
    )
    reward = jnp.einsum("pbr,rq->pbq", onehot, reward_rows, preferred_element_type=jnp.float32)
    scores = expected + reward
    inner_count = min(J, pair_count)
    grouped = scores.reshape(pair_count // inner_count, inner_count, block_rows, columns)
    highest = jnp.max(grouped, axis=1)
    totals = jnp.sum(jnp.exp(grouped - highest[:, None]), axis=1)
    return (highest.reshape(-1, columns), totals.reshape(-1, columns))


def shards_split(transitions, col_block, reward_class, reward_table, terminal):
    devices = lax.axis_size("choice")
    pair_count = transitions.shape[0]
    inner_count = min(J, pair_count)
    group_size = J // inner_count
    swap_count = group_size.bit_length() - 1
    member_index = lax.axis_index("choice") % group_size
    share_rows = STATES // devices
    next_values = lax.all_gather(terminal, "choice", axis=0, tiled=True)
    result = None
    for age_index in range(AGES - 1, -1, -1):
        highest, totals = choice_partials(
            transitions, col_block, reward_class[age_index], reward_table[age_index], next_values
        )
        for bit_index in range(swap_count):
            incoming = partner((highest, totals), "choice", bit_index)
            highest, totals = combine((highest, totals), incoming)
        block_values = highest + jnp.log(totals)
        if age_index > 0:
            gathered = lax.all_gather(
                block_values.astype(jnp.bfloat16), "choice", axis=0, tiled=True
            )
            spread = gathered.astype(jnp.float32).reshape(
                devices // group_size, group_size, block_values.shape[0], block_values.shape[1]
            )
            next_values = (
                jnp.mean(spread, axis=1).astype(jnp.bfloat16).reshape(STATES, block_values.shape[1])
            )
        else:
            result = lax.dynamic_slice_in_dim(
                block_values, member_index * share_rows, share_rows, 0
            )
    return result


UNROLL = 32
FOLD = 2
ZLAG = 3
XLAG = 5
PIECE = 16
LOWEST = -3.0e38
MESH = pl.DeviceIdType.MESH


class Plan:
    def __init__(self, rows):
        self.rows = rows
        self.group = lax.axis_index("groups")
        me = lax.axis_index("choice")
        self.core, self.x, self.z = me % 2, (me // 2) % 2, me // 4
        self.depth = lax.axis_size("choice") // 4
        self.across = self.place(self.z, 1 - self.x, self.core)
        self.beside = self.place(self.z, self.x, 1 - self.core)
        self.mates = [self.place((self.z + d) % self.depth, self.x, self.core) for d in range(1, self.depth)]

    def place(self, z, x, core):
        return z * 4 + x * 2 + core

    def column(self, x, core, b):
        return ((x * 2 + core) * self.rows + b) * self.depth

    def own(self, b):
        return self.column(self.x, self.core, b) + self.z

    def greet(self):
        barrier = pltpu.get_barrier_semaphore()
        near = self.mates + [self.across, self.beside]
        for target in near:
            pl.semaphore_signal(barrier, inc=1, device_id=(self.group, target), device_id_type=MESH)
        pl.semaphore_wait(barrier, len(near))


class Gather:
    def __init__(self, plan, values, side, sems):
        self.plan, self.values, self.side = plan, values, side
        self.send, self.zrecv, self.xrecv, self.zlast, self.xlast, self.brecv = sems

    def copy(self, start, count, recv, target):
        block = self.values.at[pl.ds(start, count)]
        return pltpu.make_async_remote_copy(
            src_ref=block, dst_ref=block, send_sem=self.send.at[self.side], recv_sem=recv,
            device_id=(self.plan.group, target), device_id_type=MESH,
        )

    def take(self, count, sem):
        block = self.values.at[pl.ds(0, count)]
        pltpu.make_async_copy(block, block, sem).wait()

    def aside(self, start, count):
        self.copy(start, count, self.brecv.at[self.side], self.plan.beside).start()

    def spread(self, b):
        p = self.plan
        for target in p.mates:
            self.copy(p.own(b), 1, self.zrecv.at[self.side, b], target).start()

    def along(self, b):
        p = self.plan
        if p.depth > 1:
            self.take(p.depth - 1, self.zrecv.at[self.side, b])
        mine = p.column(p.x, p.core, b)
        self.copy(mine, p.depth, self.xrecv.at[self.side, b], p.across).start()
        self.aside(mine, p.depth)

    def over(self, b):
        p = self.plan
        self.take(p.depth, self.xrecv.at[self.side, b])
        self.aside(p.column(1 - p.x, p.core, b), p.depth)

    def last_spread(self):
        p = self.plan
        own = p.own(p.rows - 1)
        self.copy(own, 1, self.xlast.at[self.side, 0], p.across).start()
        for i, target in enumerate(p.mates):
            self.copy(own, 1, self.zlast.at[self.side, i], target).start()
        self.aside(own, 1)

    def last_along(self, i):
        p = self.plan
        self.take(1, self.zlast.at[self.side, i])
        block = p.column(p.x, p.core, p.rows - 1) + (p.z + p.depth - 1 - i) % p.depth
        self.copy(block, 1, self.xlast.at[self.side, i + 1], p.across).start()
        self.aside(block, 1)

    def last_over(self, i):
        p = self.plan
        self.take(1, self.xlast.at[self.side, i])
        block = p.column(1 - p.x, p.core, p.rows - 1) + (p.z + p.depth - i) % p.depth
        self.aside(block, 1)

    def finish(self):
        p = self.plan
        self.take(2 * p.rows * p.depth, self.brecv.at[self.side])
        self.take((4 * p.depth - 1) * p.rows, self.send.at[self.side])


def lookup(pair, age, class_ref, table_ref, reward_ref):
    types, size = table_ref.shape[1], class_ref.shape[2]
    classes = class_ref[age, pl.ds(pair, PIECE), :]
    table = table_ref[age]
    kinds = lax.broadcasted_iota(jnp.int32, (types, size), 0)
    for i in range(PIECE):
        onehot = jnp.where(classes[i : i + 1, :] == kinds, 1.0, 0.0).astype(jnp.bfloat16)
        reward_ref[pair + i] = lax.dot_general(
            onehot, table, (((0,), (0,)), ((), ())), preferred_element_type=jnp.float32
        ).astype(jnp.bfloat16)


def chunk(pair, age, cols_ref, trans, class_ref, table_ref, reward_ref, values, high_ref, total_ref):
    depth, size = trans.shape[1], trans.shape[2]
    types = table_ref.shape[1]
    classes = class_ref[age, pl.ds(pair, UNROLL), :]
    table = table_ref[age]
    kinds = lax.broadcasted_iota(jnp.int32, (types, size), 0)
    for first in range(0, UNROLL, FOLD):
        scores = []
        for i in range(first, first + FOLD):
            left = jnp.concatenate([trans[pair + i, k] for k in range(depth)], axis=1)
            right = jnp.concatenate([values[cols_ref[(pair + i) * depth + k]] for k in range(depth)], axis=0)
            score = jnp.dot(left, right, preferred_element_type=jnp.float32)
            if reward_ref is None:
                onehot = jnp.where(classes[i : i + 1, :] == kinds, 1.0, 0.0).astype(jnp.bfloat16)
                score = score + lax.dot_general(
                    onehot, table, (((0,), (0,)), ((), ())), preferred_element_type=jnp.float32
                )
            else:
                score = score + reward_ref[pair + i].astype(jnp.float32)
            scores.append(score)
        before = high_ref[...]
        high = before
        for s in scores:
            high = jnp.maximum(high, s)
        total = total_ref[...] * jnp.exp(before - high)
        for s in scores:
            total = total + jnp.exp(s - high)
        high_ref[...] = high
        total_ref[...] = total


def whole_kernel(
    cols_ref, trans_ref, class_ref, table_ref, own_ref, out_ref,
    trans, values0, values1, reward_ref, high_ref, total_ref, load, send, zrecv, xrecv, zlast, xlast, brecv,
):
    rows = own_ref.shape[0]
    steps = J // UNROLL
    plan = Plan(rows)
    values = (values0, values1)
    gathers = [Gather(plan, v, i, (send, zrecv, xrecv, zlast, xlast, brecv)) for i, v in enumerate(values)]

    def loading(c):
        part = pl.ds(c * UNROLL, UNROLL)
        return pltpu.make_async_copy(trans_ref.at[part], trans.at[part], load.at[c])

    plan.greet()
    first = gathers[0]

    def begin(b):
        values0[plan.own(b)] = own_ref[b]
        if b == rows - 1:
            first.last_spread()
        else:
            first.spread(b)

    early = rows // 2
    pieces = early * J // PIECE

    def look(age, first_part, last_part):
        @pl.loop(pieces * first_part // 6, pieces * last_part // 6)
        def _(c):
            lookup(c * PIECE, age, class_ref, table_ref, reward_ref)

    for b in range(min(2, rows)):
        begin(b)

    @pl.loop(0, rows * steps)
    def _(c):
        loading(c).start()

    look(AGES - 1, 0, 4)
    for b in range(rows - 1):
        first.along(b)
        if b + 2 < rows:
            begin(b + 2)
        if b > 0:
            first.over(b - 1)
        if b == 0:
            look(AGES - 1, 4, 6)
    for i in range(plan.depth - 1):
        first.last_along(i)
    if rows > 1:
        first.over(rows - 2)
    for i in range(plan.depth):
        first.last_over(i)
    first.finish()

    for turn in range(AGES):
        age = AGES - 1 - turn
        held = values[turn % 2]
        ahead = gathers[(turn + 1) % 2]
        last = turn == AGES - 1

        def row(r, rewards):
            high_ref[...] = jnp.full_like(high_ref, LOWEST)
            total_ref[...] = jnp.zeros_like(total_ref)

            @pl.loop(0, steps)
            def _(q):
                if turn == 0:
                    loading(r * steps + q).wait()
                chunk(
                    (r * steps + q) * UNROLL, age, cols_ref, trans, class_ref, table_ref, rewards,
                    held, high_ref, total_ref,
                )
                if not last:
                    at = r * steps + q

                    @pl.when((at % steps == (steps - 1 + ZLAG) % steps) & (at >= steps - 1 + ZLAG))
                    def _():
                        ahead.along((at - ZLAG) // steps)

                    @pl.when((at % steps == (steps - 1 + XLAG) % steps) & (at >= steps - 1 + XLAG))
                    def _():
                        ahead.over((at - XLAG) // steps)

            done = high_ref[...] + jnp.log(total_ref[...])
            if last:
                out_ref[r] = done
            else:
                ahead.values[plan.own(r)] = done.astype(jnp.bfloat16)

        @pl.loop(0, early)
        def _(r):
            row(r, reward_ref)
            if not last:
                ahead.spread(r)

        @pl.loop(early, rows)
        def _(r):
            row(r, None)
            if not last:

                @pl.when(r < rows - 1)
                def _():
                    ahead.spread(r)

                @pl.when(r == rows - 1)
                def _():
                    ahead.last_spread()

        if not last:
            ends = [steps * (b + 1) - 1 for b in range(rows - 1)]
            final = rows * steps - 1
            for b, end in enumerate(ends):
                if end + ZLAG > final:
                    ahead.along(b)
            look(age - 1, 0, 3)
            for i in range(plan.depth - 1):
                ahead.last_along(i)
            look(age - 1, 3, 4)
            for b, end in enumerate(ends):
                if end + XLAG > final:
                    ahead.over(b)
            look(age - 1, 4, 6)
            for i in range(plan.depth):
                ahead.last_over(i)
            ahead.finish()


def shards_whole(transitions, col_block, reward_class, reward_table, terminal):
    pairs, depth, size, _ = transitions.shape
    columns = terminal.shape[1]
    devices = lax.axis_size("choice")
    blocks = devices * (terminal.shape[0] // size)
    rows = pairs // J
    ranks = devices // 4
    owner, b = col_block // rows, col_block % rows
    cols = ((owner % 4) * rows + b) * ranks + owner // 4
    vmem = pl.BlockSpec(memory_space=pltpu.VMEM)
    out = pl.pallas_call(
        whole_kernel,
        out_shape=jax.ShapeDtypeStruct((rows, size, columns), jnp.float32),
        in_specs=[
            pl.BlockSpec(memory_space=pltpu.SMEM), pl.BlockSpec(memory_space=pl.ANY), vmem, vmem, vmem,
        ],
        out_specs=vmem,
        scratch_shapes=[
            pltpu.VMEM(transitions.shape, jnp.bfloat16),
            pltpu.VMEM((blocks, size, columns), jnp.bfloat16),
            pltpu.VMEM((blocks, size, columns), jnp.bfloat16),
            pltpu.VMEM((max(rows // 2, 1) * J, size, columns), jnp.bfloat16),
            pltpu.VMEM((size, columns), jnp.float32),
            pltpu.VMEM((size, columns), jnp.float32),
            pltpu.SemaphoreType.DMA((pairs // UNROLL,)),
            pltpu.SemaphoreType.DMA((2,)),
            pltpu.SemaphoreType.DMA((2, rows)),
            pltpu.SemaphoreType.DMA((2, rows)),
            pltpu.SemaphoreType.DMA((2, ranks)),
            pltpu.SemaphoreType.DMA((2, ranks)),
            pltpu.SemaphoreType.DMA((2,)),
        ],
        compiler_params=pltpu.CompilerParams(
            collective_id=0, has_side_effects=True, vmem_limit_bytes=58 << 20
        ),
        cost_estimate=pl.CostEstimate(
            flops=2 * AGES * pairs * (depth * size + reward_table.shape[1]) * size * columns,
            bytes_accessed=transitions.size * 2,
            transcendentals=AGES * pairs * size * columns,
        ),
    )(cols.reshape(-1), transitions, reward_class, reward_table, terminal.reshape(rows, size, columns))
    return out.reshape(terminal.shape)


def shards(transitions, col_block, reward_class, reward_table, terminal):
    whole = transitions.shape[0] % J == 0 and lax.axis_size("choice") % 4 == 0
    body = shards_whole if whole else shards_split
    return body(transitions, col_block, reward_class, reward_table, terminal)


def solution(mesh):
    return jax.shard_map(
        shards,
        mesh=mesh,
        in_specs=(
            P("choice", None, None, None),
            P("choice", None),
            P(None, "choice", None),
            P(None, None, "groups"),
            P("choice", "groups"),
        ),
        out_specs=P("choice", "groups"),
        check_vma=False,
    )
```
